32 devices in a mesh: rows: 8 (over y, x, core), cols: 4 (over z).
Axes of the slice: x: 2, y: 2, z: 4, core: 2. Of those that a mesh axis runs over, the one named last changes fastest.
Arguments:
- grad: bfloat16 [28672, 8192], P(('rows', 'cols')), may hold values from -8 to 8
- momentum: float32 [28672, 8192], P('rows', 'cols'), may hold values from -8 to 8
- right_basis: bfloat16 [8192, 512], P('cols'), may hold values from -0.0625 to 0.0625
Outputs:
- momentum_new: float32 [28672, 8192], P('rows', 'cols')
- left_factor: float32 [28672, 512], P('rows')
- right_new: bfloat16 [8192, 512], P('cols')
The draws below stay inside these ranges and needn't reach their ends.
All inputs are finite; a program needn't handle non-finite values.
Results may differ from the reference program's by a relative error of at most 0.01225.
Values may be sent and summed in bfloat16 or wider, within the bound.
A program may use at most 192 MiB of HBM per device.

```python
import math
import jax
import jax.numpy as jnp
from jax import lax

OUT_DIM = 28672
IN_DIM = 8192
RANK = 512


def shared_part(key):
    base = jax.random.fold_in(key, 101)
    key_left, key_right, key_strength = jax.random.split(base, 3)
    width = max(1, RANK // 4)
    strength = jnp.exp(jax.random.uniform(key_strength, (width,), jnp.float32, math.log(0.5), math.log(2.0)))
    left_part = jax.random.normal(key_left, (OUT_DIM, width), jnp.float32)
    right_part = jax.random.normal(key_right, (IN_DIM, width), jnp.float32)
    left_part = left_part * (strength / math.sqrt(width))
    return jnp.dot(left_part, right_part.T, precision=lax.Precision.HIGHEST)


def own_noise(key, salt):
    noise_key = jax.random.fold_in(key, salt)
    noise = jax.random.normal(noise_key, (OUT_DIM, IN_DIM), jnp.float32)
    return 0.35 * noise


def column_ramp():
    position = jnp.arange(IN_DIM, dtype=jnp.float32) / float(IN_DIM)
    low_end = 0.6
    high_end = 1.8
    ramp = low_end * jnp.exp(position * math.log(high_end / low_end))
    return ramp[None, :]


def draw_grad(key, part):
    values = (0.5 * shared_part(key) + own_noise(key, 211)) * column_ramp()
    return jnp.clip(values, -8.0, 8.0).astype(jnp.bfloat16)


def draw_momentum(key, part):
    values = (0.7 * shared_part(key) + own_noise(key, 223)) * column_ramp()
    return jnp.clip(values, -8.0, 8.0).astype(jnp.float32)


def steps_of(stream_key, dims, shards, low, top_value):
    def one(dim, blocks):
        heights = jax.random.uniform(jax.random.fold_in(jax.random.fold_in(stream_key, 6), dim), (blocks,), jnp.float32, low / len(shards), top_value / len(shards))
        return jnp.repeat(jnp.exp(heights), dims[dim] // blocks).reshape((-1,) + (1,) * (len(dims) - dim - 1))

    factor_of = one(*shards[0])
    for cut in shards[1:]:
        factor_of = factor_of * one(*cut)
    return factor_of


def centred(key, extent, deviation, reach, pieces=(), kind=jnp.bfloat16):
    drawn = jax.random.normal(key, extent, jnp.float32) * deviation
    if len(pieces) > 0:
        drawn = steps_of(key, extent, pieces, -0.22, 0.18) * drawn
    return jnp.clip(drawn, min=-reach, max=reach).astype(kind)


def setup_inputs(seed: int = 0) -> dict:
    seeds = jax.random.split(jax.random.key(seed), 4)
    return {
        "grad": draw_grad(jax.random.fold_in(seeds[3], 71), 0),
        "momentum": draw_momentum(jax.random.fold_in(seeds[3], 71), 0),
        "right_basis": centred(seeds[2], (IN_DIM, RANK), IN_DIM ** -0.5, 0.0625, ((0, 4),)),
    }


def reference(grad, momentum, right_basis):
    blend = momentum + grad.astype(jnp.float32)
    blend_half = blend.astype(jnp.bfloat16)
    panel = jnp.dot(blend_half.astype(jnp.float32), right_basis.astype(jnp.float32), preferred_element_type=jnp.float32)
    gram_total = jnp.dot(panel.T, panel, precision=lax.Precision.HIGHEST)
    lower_factor = jnp.linalg.cholesky(gram_total)
    left_factor = jax.scipy.linalg.solve_triangular(lower_factor, panel.T, lower=True).T
    left_half = left_factor.astype(jnp.bfloat16)
    projected = jnp.dot(blend_half.T.astype(jnp.float32), left_half.astype(jnp.float32), preferred_element_type=jnp.float32)
    projected_half = projected.astype(jnp.bfloat16)
    feedback = jnp.dot(left_half.astype(jnp.float32), projected_half.T.astype(jnp.float32), preferred_element_type=jnp.float32)
    momentum_new = blend - 0.05 * feedback
    column_sums = lax.optimization_barrier(jnp.sum(projected * projected, axis=0))
    right_new = (projected / jnp.sqrt(column_sums + 1e-06)).astype(jnp.bfloat16)
    return (momentum_new, left_factor, right_new)
```

```python
import jax
import jax.numpy as jnp
from jax import lax
from jax.sharding import PartitionSpec as P

epsilon = 1e-06
feedback_weight = 0.05


def shift(x, s):
    n = lax.axis_size("cols")
    return lax.ppermute(x, "cols", [(i, (i + s) % n) for i in range(n)])


def flip(x, axis, stride):
    return lax.ppermute(x, axis, [(i, i ^ stride) for i in range(lax.axis_size(axis))])


def sum_everywhere(x):
    levels = lax.axis_size("rows").bit_length() - 1
    index = lax.axis_index("rows")
    for level in range(levels):
        bit = (index >> level) & 1
        half = x.shape[0] // 2
        keep = lax.dynamic_slice_in_dim(x, bit * half, half)
        send = lax.dynamic_slice_in_dim(x, (1 - bit) * half, half)
        x = keep + flip(send, "rows", 1 << level)
    for level in range(lax.axis_size("cols").bit_length() - 1):
        x = x + flip(x, "cols", 1 << level)
    for level in reversed(range(levels)):
        bit = (index >> level) & 1
        other = flip(x, "rows", 1 << level)
        low = jnp.where(bit == 0, x, other)
        high = jnp.where(bit == 0, other, x)
        x = jnp.concatenate([low, high], axis=0)
    return x


def local(grad, momentum, right_basis):
    n = lax.axis_size("cols")
    me = lax.axis_index("cols")
    deep = grad.shape[0]
    width = momentum.shape[1]
    order = sorted(range(1, n), key=lambda s: -min(s, n - s))
    tile = lambda c: lax.dynamic_slice(grad, (0, c * width), (deep, width))
    pieces = {0: tile(me)}
    for s in order:
        pieces[s] = shift(tile((me + s) % n), s)
    regrouped = jnp.zeros((n * deep, width), grad.dtype)
    blend_half = jnp.zeros((n * deep, width), jnp.bfloat16)
    panel_own = None
    for s in [0] + order:
        source = (me - s + n) % n
        chunk = lax.dynamic_slice_in_dim(momentum, source * deep, deep) + pieces[s].astype(jnp.float32)
        chunk = chunk.astype(jnp.bfloat16)
        partial = jnp.dot(chunk, right_basis, preferred_element_type=jnp.float32)
        regrouped = lax.dynamic_update_slice_in_dim(regrouped, pieces[s], source * deep, 0)
        blend_half = lax.dynamic_update_slice_in_dim(blend_half, chunk, source * deep, 0)
        if s == 0:
            panel_own = partial
        else:
            panel_own = panel_own + shift(partial.astype(jnp.bfloat16), -s).astype(jnp.float32)
    gram = sum_everywhere(jnp.dot(panel_own.T, panel_own, precision=lax.Precision.HIGHEST))
    panel = jnp.zeros((n * deep, panel_own.shape[1]), jnp.float32)
    panel = lax.dynamic_update_slice_in_dim(panel, panel_own, me * deep, 0)
    for s in range(1, n):
        panel = lax.dynamic_update_slice_in_dim(panel, shift(panel_own, s), (me - s + n) % n * deep, 0)
    lower_factor = jnp.linalg.cholesky(gram)
    left_factor = jax.scipy.linalg.solve_triangular(lower_factor, panel.T, lower=True).T
    left_half = left_factor.astype(jnp.bfloat16)
    contract_rows = (((0,), (0,)), ((), ()))
    term = lax.dot_general(blend_half, left_half, contract_rows, preferred_element_type=jnp.float32)
    projected = lax.psum(term.astype(jnp.bfloat16), "rows").astype(jnp.float32)
    column_sums = lax.psum(jnp.sum(projected * projected, axis=0), "cols")
    projected_half = projected.astype(jnp.bfloat16)
    right_new = (projected / jnp.sqrt(column_sums + epsilon)).astype(jnp.bfloat16)
    contract_cols = (((1,), (1,)), ((), ()))
    feedback = lax.dot_general(
        left_half, projected_half, contract_cols, preferred_element_type=jnp.float32
    )
    blend = momentum + regrouped.astype(jnp.float32)
    momentum_new = blend - feedback_weight * feedback
    return (momentum_new, left_factor, right_new)


def solution(mesh):
    placed = (P(("rows", "cols"), None), P("rows", "cols"), P("cols", None))
    return jax.shard_map(
        local,
        mesh=mesh,
        in_specs=placed,
        out_specs=(P("rows", "cols"), P("rows", None), P("cols", None)),
        check_vma=False,
    )
```

```python
import jax
import jax.numpy as jnp
from jax import lax
from jax.experimental import pallas as pl
from jax.experimental.pallas import tpu as pltpu
from jax.sharding import PartitionSpec as P

epsilon = 1e-06
feedback_weight = 0.05


BLOCK = 128
HIGHEST = lax.Precision.HIGHEST


def rows_with(x, y, dims):
    return lax.dot_general(x, y, (dims, ((), ())), precision=HIGHEST, preferred_element_type=jnp.float32)


def factor_block(tile):
    lane = lax.broadcasted_iota(jnp.int32, (8, BLOCK), 1)
    row = lax.broadcasted_iota(jnp.int32, (8, 2 * BLOCK), 0)
    row_half = row[:, :BLOCK]

    def group(g, carry):
        base = pl.multiple_of(g * 8, 8)
        block = tile[pl.ds(base, 8), :]
        left = block[:, :BLOCK]
        columns = [
            jnp.broadcast_to(jnp.sum(jnp.where(lane == base + j, left, 0.0), axis=1, keepdims=True), (8, BLOCK))
            for j in range(8)
        ]
        for i in range(8):
            pivot = columns[i][i:i + 1, :]
            scale = lax.rsqrt(pivot)
            scale = scale * (1.5 - 0.5 * pivot * scale * scale)
            multiplier = columns[i] * scale
            wide = jnp.concatenate([multiplier, multiplier], axis=1)
            wide_scale = jnp.concatenate([scale, scale], axis=1)
            top = block[i:i + 1, :] * wide_scale
            block = jnp.where(row > i, block - wide * top, jnp.where(row == i, top, block))
            for j in range(i + 1, 8):
                head = columns[j][i:i + 1, :] * scale
                columns[j] = jnp.where(row_half > i, columns[j] - multiplier * head, columns[j])
        tile[pl.ds(base, 8), :] = block
        below = jnp.where(lane >= base + 8, block[:, :BLOCK], 0.0).T
        change = below[:, 0:1] * block[0:1, :]
        for i in range(1, 8):
            change = change + below[:, i:i + 1] * block[i:i + 1, :]
        tile[...] = tile[...] - change
        return carry

    lax.fori_loop(0, BLOCK // 8, group, 0)


def inverse_factor_kernel(gram_ref, out_ref, work, tile):
    size = gram_ref.shape[0]
    work[...] = gram_ref[...]
    out_ref[...] = jnp.zeros_like(out_ref)
    diagonal = lax.broadcasted_iota(jnp.int32, (BLOCK, BLOCK), 0) == lax.broadcasted_iota(jnp.int32, (BLOCK, BLOCK), 1)
    for first in range(0, size, BLOCK):
        last = first + BLOCK
        tile[:, :BLOCK] = work[first:last, first:last]
        tile[:, BLOCK:] = jnp.where(diagonal, 1.0, 0.0)
        factor_block(tile)
        inverse = tile[:, BLOCK:]
        out_ref[first:last, first:last] = inverse
        if first > 0:
            out_ref[first:last, :first] = rows_with(inverse, out_ref[first:last, :first], ((1,), (0,)))
        if last < size:
            upper = rows_with(inverse, work[first:last, last:], ((1,), (0,)))
            work[last:, last:] = work[last:, last:] - rows_with(upper, upper, ((0,), (0,)))
            done = out_ref[first:last, :last]
            out_ref[last:, :last] = out_ref[last:, :last] - rows_with(upper, done, ((0,), (0,)))


def inverse_factor(gram):
    size = gram.shape[0]
    return pl.pallas_call(
        inverse_factor_kernel,
        out_shape=jax.ShapeDtypeStruct((size, size), jnp.float32),
        in_specs=[pl.BlockSpec(memory_space=pltpu.VMEM)],
        out_specs=pl.BlockSpec(memory_space=pltpu.VMEM),
        scratch_shapes=[pltpu.VMEM((size, size), jnp.float32), pltpu.VMEM((BLOCK, 2 * BLOCK), jnp.float32)],
        compiler_params=pltpu.CompilerParams(vmem_limit_bytes=16 << 20),
        cost_estimate=pl.CostEstimate(flops=80 * 10 ** 9, bytes_accessed=2 * 4 * size * size, transcendentals=0),
    )(gram)


def fresh(shape, dtype):
    return pl.pallas_call(
        lambda out_ref: None,
        out_shape=jax.ShapeDtypeStruct(shape, dtype),
        out_specs=pl.BlockSpec(memory_space=pl.ANY),
    )()


def shift(x, s):
    n = lax.axis_size("cols")
    return lax.ppermute(x, "cols", [(i, (i + s) % n) for i in range(n)])


def flip(x, axis, stride):
    return lax.ppermute(x, axis, [(i, i ^ stride) for i in range(lax.axis_size(axis))])


def sum_everywhere(x):
    levels = lax.axis_size("rows").bit_length() - 1
    index = lax.axis_index("rows")
    for level in range(levels):
        bit = (index >> level) & 1
        half = x.shape[0] // 2
        keep = lax.dynamic_slice_in_dim(x, bit * half, half)
        send = lax.dynamic_slice_in_dim(x, (1 - bit) * half, half)
        x = keep + flip(send, "rows", 1 << level)
    for level in range(lax.axis_size("cols").bit_length() - 1):
        x = x + flip(x, "cols", 1 << level)
    for level in reversed(range(levels)):
        bit = (index >> level) & 1
        other = flip(x, "rows", 1 << level)
        low = jnp.where(bit == 0, x, other)
        high = jnp.where(bit == 0, other, x)
        x = jnp.concatenate([low, high], axis=0)
    return x


def local(grad, momentum, right_basis):
    n = lax.axis_size("cols")
    me = lax.axis_index("cols")
    deep = grad.shape[0]
    width = momentum.shape[1]
    order = sorted(range(1, n), key=lambda s: -min(s, n - s))
    tile = lambda c: lax.dynamic_slice(grad, (0, c * width), (deep, width))
    outgoing = lax.optimization_barrier([tile((me + s) % n) for s in [0] + order])
    pieces = {0: outgoing[0]}
    for s, piece in zip(order, outgoing[1:]):
        pieces[s] = shift(piece, s)
    regrouped = fresh((n * deep, width), grad.dtype)
    blend_half = fresh((n * deep, width), jnp.bfloat16)
    panel_own = None
    for s in [0] + order:
        source = (me - s + n) % n
        chunk = lax.dynamic_slice_in_dim(momentum, source * deep, deep) + pieces[s].astype(jnp.float32)
        chunk = chunk.astype(jnp.bfloat16)
        partial = jnp.dot(chunk, right_basis, preferred_element_type=jnp.float32)
        regrouped = lax.dynamic_update_slice_in_dim(regrouped, pieces[s], source * deep, 0)
        blend_half = lax.dynamic_update_slice_in_dim(blend_half, chunk, source * deep, 0)
        if s == 0:
            panel_own = partial
        else:
            panel_own = panel_own + shift(partial.astype(jnp.bfloat16), -s).astype(jnp.float32)
    panel_own = panel_own.astype(jnp.bfloat16)
    gram_own = lax.dot_general(panel_own, panel_own, (((0,), (0,)), ((), ())), preferred_element_type=jnp.float32)
    gram = sum_everywhere(gram_own)
    gram, panel_own = lax.optimization_barrier((gram, panel_own))
    arrived = {0: panel_own}
    for s in range(1, n):
        arrived[s] = shift(panel_own, s)
    inverse = inverse_factor(gram)
    panel = fresh((n * deep, panel_own.shape[1]), jnp.bfloat16)
    for s in range(n):
        panel = lax.dynamic_update_slice_in_dim(panel, arrived[s], (me - s + n) % n * deep, 0)
    left_factor = lax.dot_general(
        panel.astype(jnp.float32), inverse, (((1,), (1,)), ((), ())), precision=HIGHEST, preferred_element_type=jnp.float32
    )
    left_half = left_factor.astype(jnp.bfloat16)
    contract_rows = (((0,), (0,)), ((), ()))
    term = lax.dot_general(blend_half, left_half, contract_rows, preferred_element_type=jnp.float32)
    projected = lax.psum(term.astype(jnp.bfloat16), "rows").astype(jnp.float32)
    column_sums = lax.psum(jnp.sum(projected * projected, axis=0), "cols")
    projected_half = projected.astype(jnp.bfloat16)
    right_new = (projected / jnp.sqrt(column_sums + epsilon)).astype(jnp.bfloat16)
    contract_cols = (((1,), (1,)), ((), ()))
    feedback = lax.dot_general(
        left_half, projected_half, contract_cols, preferred_element_type=jnp.float32
    )
    blend = momentum + regrouped.astype(jnp.float32)
    momentum_new = blend - feedback_weight * feedback
    return (momentum_new, left_factor, right_new)


def solution(mesh):
    placed = (P(("rows", "cols"), None), P("rows", "cols"), P("cols", None))
    return jax.shard_map(
        local,
        mesh=mesh,
        in_specs=placed,
        out_specs=(P("rows", "cols"), P("rows", None), P("cols", None)),
        check_vma=False,
    )
```

```python
import jax
import jax.numpy as jnp
from jax import lax
from jax.experimental import pallas as pl
from jax.experimental.pallas import tpu as pltpu
from jax.sharding import PartitionSpec as P

epsilon = 1e-06
feedback_weight = 0.05


BLOCK = 128
HIGHEST = lax.Precision.HIGHEST


def rows_with(x, y, dims):
    return lax.dot_general(x, y, (dims, ((), ())), precision=HIGHEST, preferred_element_type=jnp.float32)


def factor_block(tile):
    lane = lax.broadcasted_iota(jnp.int32, (8, BLOCK), 1)
    row = lax.broadcasted_iota(jnp.int32, (8, 2 * BLOCK), 0)
    row_half = row[:, :BLOCK]

    def group(g, carry):
        base = pl.multiple_of(g * 8, 8)
        block = tile[pl.ds(base, 8), :]
        left = block[:, :BLOCK]
        columns = [
            jnp.broadcast_to(jnp.sum(jnp.where(lane == base + j, left, 0.0), axis=1, keepdims=True), (8, BLOCK))
            for j in range(8)
        ]
        for i in range(8):
            pivot = columns[i][i:i + 1, :]
            scale = lax.rsqrt(pivot)
            scale = scale * (1.5 - 0.5 * pivot * scale * scale)
            multiplier = columns[i] * scale
            wide = jnp.concatenate([multiplier, multiplier], axis=1)
            wide_scale = jnp.concatenate([scale, scale], axis=1)
            top = block[i:i + 1, :] * wide_scale
            block = jnp.where(row > i, block - wide * top, jnp.where(row == i, top, block))
            for j in range(i + 1, 8):
                head = columns[j][i:i + 1, :] * scale
                columns[j] = jnp.where(row_half > i, columns[j] - multiplier * head, columns[j])
        tile[pl.ds(base, 8), :] = block
        below = jnp.where(lane >= base + 8, block[:, :BLOCK], 0.0).T
        change = below[:, 0:1] * block[0:1, :]
        for i in range(1, 8):
            change = change + below[:, i:i + 1] * block[i:i + 1, :]
        tile[...] = tile[...] - change
        return carry

    lax.fori_loop(0, BLOCK // 8, group, 0)


def inverse_factor_kernel(gram_ref, out_ref, work, tile):
    size = gram_ref.shape[0]
    work[...] = gram_ref[...]
    out_ref[...] = jnp.zeros_like(out_ref)
    diagonal = lax.broadcasted_iota(jnp.int32, (BLOCK, BLOCK), 0) == lax.broadcasted_iota(jnp.int32, (BLOCK, BLOCK), 1)
    for first in range(0, size, BLOCK):
        last = first + BLOCK
        tile[:, :BLOCK] = work[first:last, first:last]
        tile[:, BLOCK:] = jnp.where(diagonal, 1.0, 0.0)
        factor_block(tile)
        inverse = tile[:, BLOCK:]
        out_ref[first:last, first:last] = inverse
        if first > 0:
            out_ref[first:last, :first] = rows_with(inverse, out_ref[first:last, :first], ((1,), (0,)))
        if last < size:
            upper = rows_with(inverse, work[first:last, last:], ((1,), (0,)))
            work[last:, last:] = work[last:, last:] - rows_with(upper, upper, ((0,), (0,)))
            done = out_ref[first:last, :last]
            out_ref[last:, :last] = out_ref[last:, :last] - rows_with(upper, done, ((0,), (0,)))


def inverse_factor(gram):
    size = gram.shape[0]
    return pl.pallas_call(
        inverse_factor_kernel,
        out_shape=jax.ShapeDtypeStruct((size, size), jnp.float32),
        in_specs=[pl.BlockSpec(memory_space=pltpu.VMEM)],
        out_specs=pl.BlockSpec(memory_space=pltpu.VMEM),
        scratch_shapes=[pltpu.VMEM((size, size), jnp.float32), pltpu.VMEM((BLOCK, 2 * BLOCK), jnp.float32)],
        compiler_params=pltpu.CompilerParams(vmem_limit_bytes=16 << 20),
        cost_estimate=pl.CostEstimate(flops=80 * 10 ** 9, bytes_accessed=2 * 4 * size * size, transcendentals=0),
    )(gram)


def fresh(shape, dtype):
    return pl.pallas_call(
        lambda out_ref: None,
        out_shape=jax.ShapeDtypeStruct(shape, dtype),
        out_specs=pl.BlockSpec(memory_space=pl.ANY),
    )()


def shift(x, s):
    n = lax.axis_size("cols")
    return lax.ppermute(x, "cols", [(i, (i + s) % n) for i in range(n)])


def flip(x, axis, stride):
    return lax.ppermute(x, axis, [(i, i ^ stride) for i in range(lax.axis_size(axis))])


def halve(x, levels, sent):
    index = lax.axis_index("rows")
    for level in levels:
        bit = (index >> level) & 1
        half = x.shape[0] // 2
        keep = lax.dynamic_slice_in_dim(x, bit * half, half)
        send = lax.dynamic_slice_in_dim(x, (1 - bit) * half, half)
        x = keep + flip(send.astype(sent), "rows", 1 << level).astype(x.dtype)
    return x


def double(x, levels):
    index = lax.axis_index("rows")
    for level in reversed(levels):
        bit = (index >> level) & 1
        other = flip(x, "rows", 1 << level)
        low = jnp.where(bit == 0, x, other)
        high = jnp.where(bit == 0, other, x)
        x = jnp.concatenate([low, high], axis=0)
    return x


def butterfly(x, axis):
    for level in range(lax.axis_size(axis).bit_length() - 1):
        x = x + flip(x, axis, 1 << level)
    return x


def sum_everywhere(x):
    levels = list(range(lax.axis_size("rows").bit_length() - 1))
    return double(butterfly(halve(x, levels, x.dtype), "cols"), levels)


def sum_rows(x):
    levels = list(range(lax.axis_size("rows").bit_length() - 1))
    half = x.shape[0] // 2
    orders = (levels, levels[:1] + levels[:0:-1])
    parts = [halve(x[i * half:(i + 1) * half], order, jnp.bfloat16) for i, order in enumerate(orders)]
    parts = [double(part.astype(jnp.bfloat16), order) for part, order in zip(parts, orders)]
    return jnp.concatenate(parts, axis=0)


def local(grad, momentum, right_basis):
    n = lax.axis_size("cols")
    me = lax.axis_index("cols")
    deep = grad.shape[0]
    width = momentum.shape[1]
    order = sorted(range(1, n), key=lambda s: -min(s, n - s))
    tile = lambda c: lax.dynamic_slice(grad, (0, c * width), (deep, width))
    outgoing = lax.optimization_barrier([tile((me + s) % n) for s in [0] + order])
    pieces = {0: outgoing[0]}
    for s, piece in zip(order, outgoing[1:]):
        pieces[s] = shift(piece, s)
    regrouped = fresh((n * deep, width), grad.dtype)
    blend_half = fresh((n * deep, width), jnp.bfloat16)
    panel_own = None
    for s in [0] + order:
        source = (me - s + n) % n
        chunk = lax.dynamic_slice_in_dim(momentum, source * deep, deep) + pieces[s].astype(jnp.float32)
        chunk = chunk.astype(jnp.bfloat16)
        partial = jnp.dot(chunk, right_basis, preferred_element_type=jnp.float32)
        regrouped = lax.dynamic_update_slice_in_dim(regrouped, pieces[s], source * deep, 0)
        blend_half = lax.dynamic_update_slice_in_dim(blend_half, chunk, source * deep, 0)
        if s == 0:
            panel_own = partial
        else:
            panel_own = panel_own + shift(partial.astype(jnp.bfloat16), -s).astype(jnp.float32)
    panel_own = panel_own.astype(jnp.bfloat16)
    panel_own, regrouped, blend_half = lax.optimization_barrier((panel_own, regrouped, blend_half))
    gram_own = lax.dot_general(panel_own, panel_own, (((0,), (0,)), ((), ())), preferred_element_type=jnp.float32)
    gram = sum_everywhere(gram_own)
    gram, panel_own = lax.optimization_barrier((gram, panel_own))
    arrived = {0: panel_own}
    for s in range(1, n):
        arrived[s] = shift(panel_own, s)
    inverse = inverse_factor(gram)
    panel = fresh((n * deep, panel_own.shape[1]), jnp.bfloat16)
    for s in range(n):
        panel = lax.dynamic_update_slice_in_dim(panel, arrived[s], (me - s + n) % n * deep, 0)
    left_factor = lax.dot_general(
        panel.astype(jnp.float32), inverse, (((1,), (1,)), ((), ())), precision=HIGHEST, preferred_element_type=jnp.float32
    )
    left_half = left_factor.astype(jnp.bfloat16)
    contract_rows = (((0,), (0,)), ((), ()))
    term = lax.dot_general(blend_half, left_half, contract_rows, preferred_element_type=jnp.float32)
    projected = sum_rows(term).astype(jnp.float32)
    column_sums = butterfly(jnp.sum(projected * projected, axis=0), "cols")
    projected_half = projected.astype(jnp.bfloat16)
    right_new = (projected / jnp.sqrt(column_sums + epsilon)).astype(jnp.bfloat16)
    contract_cols = (((1,), (1,)), ((), ()))
    feedback = lax.dot_general(
        left_half, projected_half, contract_cols, preferred_element_type=jnp.float32
    )
    blend = momentum + regrouped.astype(jnp.float32)
    momentum_new = blend - feedback_weight * feedback
    return (momentum_new, left_factor, right_new)


def solution(mesh):
    placed = (P(("rows", "cols"), None), P("rows", "cols"), P("cols", None))
    return jax.shard_map(
        local,
        mesh=mesh,
        in_specs=placed,
        out_specs=(P("rows", "cols"), P("rows", None), P("cols", None)),
        check_vma=False,
    )
```
